128 devices in a mesh: dp: 16 (over x, z_hi, core), proto: 8 (over y, z_lo).
Axes of the slice: x: 4, y: 4, z: 4 (z_hi: 2, z_lo: 2; z = z_hi * 2 + z_lo), core: 2. Of those that a mesh axis runs over, the one named last changes fastest.
Arguments:
- student_feats: float32 [2560, 256], P('dp'), may hold values from -6 to 6
- teacher_feats: float32 [512, 256], P('dp'), may hold values from -6 to 6
- student_proto: float32 [256, 65536], P('dp', 'proto'), may hold values from -6 to 6
- teacher_proto: float32 [256, 65536], P('dp', 'proto'), may hold values from -6 to 6
- crops: int32 [2560, 2], P('dp'), may hold values from 0 to 15, as said below
- step: int32 [1], replicated, may hold values from 0 to 24999
Outputs:
- student_next: float32 [256, 65536], P('dp', 'proto')
- teacher_next: float32 [256, 65536], P('dp', 'proto')
- feature_grad: float32 [2560, 256], P('dp')
The draws below stay inside these ranges and needn't reach their ends.
Inputs may be any that keep to these rules, and one draw needn't show every extreme that they name: Within each device's block of 160 rows every pair (image i < 16, slot c < 10) appears exactly once; slots below 2 are the global crops, slot g of image i being the same crop as teacher row 2 * i + g of that block.
All inputs are finite; a program needn't handle non-finite values.
Results may differ from the reference program's by a relative error of at most 0.0003.
Values sent between devices are 32-bit elements; how exact they have to be, the bound alone decides.
No kernel may reach another device: no remote copies, remote signals or barrier semaphores. Data moves between devices by JAX's collectives and lax.ppermute only.
A program may use at most 128 MiB of HBM per device.

```python
import jax
import jax.numpy as jnp
from jax import lax

D = 256
IMG_DEV = 16
CROPS = 10
GLOBAL_CROPS = 2
ITERS = 3
WARM_STEPS = 12500
TOTAL_STEPS = 625000
IMAGES = 256
SROWS = 2560
TROWS = 512
PROTOS = 65536
N_DP = 16


def draw_crops(key, part):
    per_rows = CROPS * IMG_DEV
    blocks = SROWS // per_rows
    keys = jax.random.split(jax.random.fold_in(key, 17), blocks)
    orders = jax.vmap(lambda one: jax.random.permutation(one, per_rows))(keys)
    flat = orders.reshape(-1).astype(jnp.int32)
    return jnp.stack([flat // CROPS, flat % CROPS], axis=1).astype(jnp.int32)


def block_levels(own_key, dims, shards, low, top_value):
    loudness, own = 1.0, jax.random.fold_in(own_key, 6)
    for axis_at, shards_of in shards:
        heights = jnp.exp(jax.random.uniform(jax.random.fold_in(own, axis_at), (shards_of,), jnp.float32, low / len(shards), top_value / len(shards)))
        loudness = loudness * jnp.repeat(heights, dims[axis_at] // shards_of).reshape([-1 if axis == axis_at else 1 for axis in range(len(dims))])
    return loudness


def centred(stream_key, extent, scale, most, cuts=(), held_as=jnp.bfloat16):
    entries = scale * jax.random.normal(stream_key, extent, jnp.float32)
    if cuts:
        entries = entries * block_levels(stream_key, extent, cuts, -0.22, 0.18)
    return jnp.clip(entries, -most, most).astype(held_as)


def setup_inputs(seed: int = 0) -> dict:
    key_of = jax.random.split(jax.random.key(seed), 7)
    student_feats = centred(key_of[0], (SROWS, D), 1.0, 6.0, ((0, 16),), jnp.float32)
    teacher_feats = centred(key_of[1], (TROWS, D), 1.0, 6.0, ((0, 16),), jnp.float32)
    student_proto = centred(key_of[2], (D, PROTOS), 1.0, 6.0, ((0, 16), (1, 8)), jnp.float32)
    teacher_proto = centred(key_of[3], (D, PROTOS), 1.0, 6.0, ((0, 16), (1, 8)), jnp.float32)
    crops = draw_crops(jax.random.fold_in(key_of[6], 71), 0)
    step = jax.random.randint(key_of[5], (1,), 0, 2 * WARM_STEPS).astype(jnp.int32)
    return {"student_feats": student_feats, "teacher_feats": teacher_feats, "student_proto": student_proto, "teacher_proto": teacher_proto, "crops": crops, "step": step}


student_temp = 0.1
loss_scale = 16777216.0
norm_eps = 1e-06
square_eps = 1e-06
rate_peak = 0.05
weight_decay = 0.04
momentum_base = 0.994
highest = lax.Precision.HIGHEST

def plan(step):
    value = step[0].astype(jnp.float32)
    ramp = jnp.minimum(1.0, value / WARM_STEPS)
    rate = rate_peak * (0.25 + 0.75 * ramp)
    teacher_temp = 0.04 + 0.03 * ramp
    momentum = 1.0 - (1.0 - momentum_base) * (jnp.cos(jnp.pi * value / TOTAL_STEPS) + 1.0) * 0.5
    return (rate, teacher_temp, momentum)

def unit_rows(values):
    norm = jnp.sqrt(lax.optimization_barrier(jnp.sum(values * values, axis=1, keepdims=True)) + norm_eps)
    return (values / norm, norm)

def unit_columns(values):
    norm = jnp.sqrt(lax.optimization_barrier(jnp.sum(values * values, axis=0, keepdims=True)) + norm_eps)
    return (values / norm, norm)

def reference(student_feats, teacher_feats, student_proto, teacher_proto, crops, step):
    rate, teacher_temp, momentum = plan(step)
    student_unit, student_norm = unit_columns(student_proto)
    teacher_unit, teacher_norm = unit_columns(teacher_proto)
    t_unit, t_norm = unit_rows(teacher_feats)
    assign = jnp.exp(jnp.dot(t_unit, teacher_unit, precision=highest, preferred_element_type=jnp.float32) / teacher_temp)
    for turn in range(ITERS):
        assign = assign / lax.optimization_barrier(jnp.sum(assign, axis=0, keepdims=True))
        assign = assign / lax.optimization_barrier(jnp.sum(assign, axis=1, keepdims=True))
    s_unit, s_norm = unit_rows(student_feats)
    pair_total = GLOBAL_CROPS * (GLOBAL_CROPS - 1) + (CROPS - GLOBAL_CROPS) * GLOBAL_CROPS
    coef = loss_scale / (pair_total * IMAGES * student_temp)
    per_rows = CROPS * IMG_DEV
    per_teach = GLOBAL_CROPS * IMG_DEV
    row_blocks = s_unit.reshape(N_DP, per_rows, D)
    table_blocks = crops.reshape(N_DP, per_rows, 2)
    assign_blocks = assign.reshape(N_DP, per_teach, PROTOS)
    teach_iota = lax.broadcasted_iota(jnp.int32, (1, per_teach), 1)

    def per_device(carry, pieces):
        rows, table, local_assign = pieces
        logits = jnp.dot(rows, student_unit, precision=highest, preferred_element_type=jnp.float32) / student_temp
        expo = jnp.exp(logits)
        prob = expo / lax.optimization_barrier(jnp.sum(expo, axis=1, keepdims=True))
        same = table[:, 0:1] == teach_iota // GLOBAL_CROPS
        other = table[:, 1:2] != teach_iota % GLOBAL_CROPS
        pairs = jnp.where(same & other, 1.0, 0.0).astype(jnp.float32)
        target = jnp.dot(pairs, local_assign, precision=highest, preferred_element_type=jnp.float32)
        count = lax.optimization_barrier(jnp.sum(pairs, axis=1, keepdims=True))
        dscore = coef * (count * prob - target)
        carry = carry + jnp.dot(rows.T, dscore, precision=highest, preferred_element_type=jnp.float32)
        back = jnp.dot(dscore, student_unit.T, precision=highest, preferred_element_type=jnp.float32)
        return (carry, back)
    grad_unit, backs = lax.scan(per_device, jnp.zeros((D, PROTOS), jnp.float32), (row_blocks, table_blocks, assign_blocks))
    feature_unit = backs.reshape(SROWS, D)
    feature_grad = (feature_unit - s_unit * lax.optimization_barrier(jnp.sum(s_unit * feature_unit, axis=1, keepdims=True))) / s_norm
    along = lax.optimization_barrier(jnp.sum(student_unit * grad_unit, axis=0, keepdims=True))
    proto_grad = (grad_unit - student_unit * along) / student_norm
    square = lax.optimization_barrier(jnp.mean(proto_grad * proto_grad, axis=0, keepdims=True))
    direction = proto_grad / jnp.sqrt(square + square_eps)
    student_next = student_proto - rate * (direction + weight_decay * student_proto)
    teacher_next = momentum * teacher_proto + (1.0 - momentum) * student_next
    return (student_next, teacher_next, feature_grad)
```

```python
import jax
import jax.numpy as jnp
from jax import lax
from jax.sharding import Mesh, PartitionSpec as P

CROPS = 10
GLOBAL_CROPS = 2
ITERS = 3
WARM_STEPS = 12500
TOTAL_STEPS = 625000

student_temp = 0.1
loss_scale = 16777216.0
norm_eps = 1e-06
square_eps = 1e-06
rate_peak = 0.05
weight_decay = 0.04
momentum_base = 0.994
highest = lax.Precision.HIGHEST
high = lax.Precision.HIGH
f32 = jnp.float32

AXES = ("x", "zh", "c", "y", "zl")
DP = ("x", "zh", "c")
PROTO = ("y", "zl")
CHIPS = ("x", "zh", "y", "zl")


def dot(a, b, dims, precision=high):
    return lax.dot_general(a, b, (dims, ((), ())), precision=precision, preferred_element_type=f32)


def plan(step):
    value = step[0].astype(f32)
    ramp = jnp.minimum(1.0, value / WARM_STEPS)
    rate = rate_peak * (0.25 + 0.75 * ramp)
    teacher_temp = 0.04 + 0.03 * ramp
    momentum = 1.0 - (1.0 - momentum_base) * (jnp.cos(jnp.pi * value / TOTAL_STEPS) + 1.0) * 0.5
    return (rate, teacher_temp, momentum)


def unit_rows(values):
    norm = jnp.sqrt(jnp.sum(values * values, axis=1, keepdims=True) + norm_eps)
    return (values / norm, norm)


def unit_columns(values):
    norm = jnp.sqrt(jnp.sum(values * values, axis=0, keepdims=True) + norm_eps)
    return (values / norm, norm)


def other_core(v):
    return lax.ppermute(v, "c", ((0, 1), (1, 0)))


def from_everyone(v, axes):
    n = lax.axis_size(axes)
    copies = jnp.broadcast_to(v, (n, *v.shape))
    return lax.all_to_all(copies, axes, split_axis=0, concat_axis=0, tiled=True)


def everywhere(v):
    v = v + other_core(v)
    return jnp.sum(from_everyone(v, CHIPS), axis=0)


def shifted(v, axis, by):
    n = lax.axis_size(axis)
    return lax.ppermute(v, axis, [(i, (i + by) % n) for i in range(n)])


def staged(v):
    for axis in ("x", "y", ("zh", "zl")):
        v = v + shifted(v, axis, 1) + shifted(v, axis, 3) + shifted(v, axis, 2)
    return v + other_core(v)


def body(student_feats, teacher_feats, student_proto, teacher_proto, crops, step):
    rate, teacher_temp, momentum = plan(step)
    n_dp = lax.axis_size(DP)
    n_proto = lax.axis_size(PROTO)
    own_rows, own_cols = student_proto.shape
    cols = own_cols // n_dp
    width = own_rows * n_dp
    crop_rows = student_feats.shape[0]
    teach_rows = teacher_feats.shape[0]
    images = teach_rows // GLOBAL_CROPS

    t_unit, _ = unit_rows(teacher_feats)
    s_unit, s_norm = unit_rows(student_feats)
    place = crops[:, 1] * images + crops[:, 0]
    q_iota = lax.broadcasted_iota(jnp.int32, (crop_rows, crop_rows), 0)
    sort = (q_iota == place[None, :]).astype(f32)
    s_sorted = dot(sort, s_unit, ((1,), (0,)), highest)

    def exchange(proto, rows):
        pieces = proto.reshape(own_rows, n_dp, cols).transpose(1, 0, 2)
        both = jnp.concatenate(
            [pieces, jnp.broadcast_to(rows, (n_dp, *rows.shape))], axis=1
        )
        got = lax.all_to_all(both, DP, split_axis=0, concat_axis=0, tiled=True)
        return got[:, :own_rows].reshape(width, cols), got[:, own_rows:]

    teach, t_all = exchange(teacher_proto, t_unit.reshape(images, GLOBAL_CROPS * width))
    student, s_all = exchange(student_proto, s_sorted.reshape(crop_rows // 2, 2 * width))

    teacher_unit, _ = unit_columns(teach)
    t_rows = jnp.concatenate([t_all[:, :, :width], t_all[:, :, width:]], axis=0).reshape(
        GLOBAL_CROPS * n_dp * images, width
    )
    kernel = jnp.exp(dot(t_rows, teacher_unit, ((1,), (0,))) / teacher_temp)
    row = None
    for turn in range(ITERS):
        if row is None:
            col = 1.0 / jnp.sum(kernel, axis=0)
        else:
            col = 1.0 / jnp.sum(kernel * row[:, None], axis=0)
        if turn == ITERS - 1:
            last = kernel * col[None, :]
            part = jnp.sum(last, axis=1)
        else:
            part = jnp.sum(kernel * col[None, :], axis=1)
        row = 1.0 / everywhere(part)

    student_unit, student_norm = unit_columns(student)
    s_rows = s_all.reshape(n_dp * crop_rows, width)
    expo = jnp.exp(dot(s_rows, student_unit, ((1,), (0,))) / student_temp)
    total = staged(jnp.sum(expo, axis=1).reshape(-1, 128)).reshape(n_dp, CROPS, images)
    pair_total = GLOBAL_CROPS * (GLOBAL_CROPS - 1) + (CROPS - GLOBAL_CROPS) * GLOBAL_CROPS
    coef = loss_scale / (pair_total * images * n_dp * student_temp)
    slots = lax.broadcasted_iota(jnp.int32, (1, CROPS, 1), 1)
    count = jnp.where(slots < GLOBAL_CROPS, GLOBAL_CROPS - 1.0, GLOBAL_CROPS * 1.0)
    scale = coef * count / total

    back_s = dot(expo, student_unit, ((1,), (1,))).reshape(n_dp, crop_rows, width)
    back_t = dot(last, student_unit, ((1,), (1,))).reshape(GLOBAL_CROPS, n_dp, images, width)
    back_t = back_t.transpose(1, 0, 2, 3).reshape(n_dp, teach_rows, width)

    def scattered(v):
        mine = jnp.sum(lax.all_to_all(v, DP, split_axis=0, concat_axis=0, tiled=True), axis=0)
        return jnp.sum(from_everyone(mine, PROTO), axis=0)

    mine_s = scattered(back_s)
    mine_t = scattered(back_t)
    me = lax.axis_index(DP)
    my_scale = lax.dynamic_index_in_dim(scale, me, 0, keepdims=False)
    row_blocks = row.reshape(GLOBAL_CROPS, n_dp, images)
    my_row = lax.dynamic_index_in_dim(row_blocks, me, 1, keepdims=False)
    part_t = coef * my_row[:, :, None] * mine_t.reshape(GLOBAL_CROPS, images, width)
    both_t = part_t[0] + part_t[1]
    target = jnp.concatenate(
        [part_t[1][None], part_t[0][None], jnp.broadcast_to(both_t, (CROPS - GLOBAL_CROPS, *both_t.shape))]
    ).reshape(crop_rows, width)
    feature_sorted = mine_s * my_scale.reshape(crop_rows, 1) - target
    feature_unit = dot(sort, feature_sorted, ((0,), (0,)), highest)
    feature_grad = (
        feature_unit - s_unit * jnp.sum(s_unit * feature_unit, axis=1, keepdims=True)
    ) / s_norm

    scaled = s_rows * scale.reshape(-1, 1)
    grad_s = dot(scaled, expo, ((0,), (0,)))
    by_slot = s_all.reshape(n_dp, CROPS, images, width)
    local = jnp.sum(by_slot[:, GLOBAL_CROPS:], axis=1)
    weights = jnp.stack([by_slot[:, 1] + local, by_slot[:, 0] + local]).reshape(-1, width)
    grad_t = dot(weights * (coef * row)[:, None], last, ((0,), (0,)))
    grad = grad_s - grad_t
    along = jnp.sum(student_unit * grad, axis=0, keepdims=True)
    proto_grad = (grad - student_unit * along) / student_norm
    square = jnp.mean(proto_grad * proto_grad, axis=0, keepdims=True)
    direction = proto_grad / jnp.sqrt(square + square_eps)
    next_cols = student - rate * (direction + weight_decay * student)
    back = lax.all_to_all(
        next_cols.reshape(n_dp, own_rows, cols), DP, split_axis=0, concat_axis=0, tiled=True
    )
    student_next = back.transpose(1, 0, 2).reshape(own_rows, own_cols)
    teacher_next = momentum * teacher_proto + (1.0 - momentum) * student_next
    return (student_next, teacher_next, feature_grad)


def solution(mesh):
    n_x, n_zh, n_c, n_y, n_zl = 4, 2, 2, 4, 2
    fine = Mesh(mesh.devices.reshape(n_x, n_zh, n_c, n_y, n_zl), AXES)
    in_specs = (P(DP, None), P(DP, None), P(DP, PROTO), P(DP, PROTO), P(DP, None), P())
    out_specs = (P(DP, PROTO), P(DP, PROTO), P(DP, None))
    return jax.shard_map(body, mesh=fine, in_specs=in_specs, out_specs=out_specs, check_vma=False)
```

```python
import functools

import jax
import jax.numpy as jnp
from jax import lax
from jax.experimental import pallas as pl
from jax.experimental.pallas import tpu as pltpu
from jax.sharding import Mesh, PartitionSpec as P

CROPS = 10
GLOBAL_CROPS = 2
WARM_STEPS = 12500
TOTAL_STEPS = 625000

student_temp = 0.1
loss_scale = 16777216.0
norm_eps = 1e-06
square_eps = 1e-06
rate_peak = 0.05
weight_decay = 0.04
momentum_base = 0.994
highest = lax.Precision.HIGHEST
high = lax.Precision.HIGH
f32 = jnp.float32
bf16 = jnp.bfloat16


AXES = ("x", "zh", "c", "y", "zl")
DP = ("x", "zh", "c")
PROTO = ("y", "zl")
CHIPS = ("x", "zh", "y", "zl")


def dot(a, b, dims, precision=high):
    return lax.dot_general(a, b, (dims, ((), ())), precision=precision, preferred_element_type=f32)


def plan(step):
    value = step[0].astype(f32)
    ramp = jnp.minimum(1.0, value / WARM_STEPS)
    rate = rate_peak * (0.25 + 0.75 * ramp)
    teacher_temp = 0.04 + 0.03 * ramp
    momentum = 1.0 - (1.0 - momentum_base) * (jnp.cos(jnp.pi * value / TOTAL_STEPS) + 1.0) * 0.5
    return (rate, teacher_temp, momentum)


NN = ((1,), (0,))
NT = ((1,), (1,))


def halves(v):
    high_part = v.astype(bf16)
    return high_part, (v - high_part.astype(f32)).astype(bf16)


def mul(a, b, dims):
    return lax.dot_general(a, b, (dims, ((), ())), preferred_element_type=f32)


def mul3(a, b, dims):
    return mul(a[0], b[0], dims) + mul(a[0], b[1], dims) + mul(a[1], b[0], dims)


def exact_pick(pick, v):
    one = v.astype(bf16)
    rest = v - one.astype(f32)
    two = rest.astype(bf16)
    three = (rest - two.astype(f32)).astype(bf16)
    return mul(pick, one, NN) + mul(pick, two, NN) + mul(pick, three, NN)


VMEM = pl.BlockSpec(memory_space=pltpu.VMEM)
SMEM = pl.BlockSpec(memory_space=pltpu.SMEM)
HBM = pl.BlockSpec(memory_space=pltpu.HBM)
DMA = pltpu.SemaphoreType.DMA


def shape(*dims):
    return jax.ShapeDtypeStruct(dims, f32)


def room_for(*dims):
    return pltpu.VMEM(dims, f32)


def call(kernel, ins, outs, scratch=(), room=16000):
    return pl.pallas_call(
        kernel,
        in_specs=ins,
        out_specs=[spec for spec, _ in outs],
        out_shape=[out for _, out in outs],
        scratch_shapes=list(scratch),
        compiler_params=pltpu.CompilerParams(vmem_limit_bytes=room * 1024),
    )


def begin(src, dst, sem):
    copy = pltpu.make_async_copy(src, dst, sem)
    copy.start()
    return copy


def rows_kernel(turn, place, sf, tf, out, s_v, t_v):
    t = tf[...]
    t = t / jnp.sqrt(jnp.sum(t * t, axis=1, keepdims=True) + norm_eps)
    n = t.shape[0]
    q = lax.broadcasted_iota(jnp.int32, (n, n), 0)
    r = lax.broadcasted_iota(jnp.int32, (n, n), 1)
    half = n // GLOBAL_CROPS
    t_v[...] = exact_pick((r == GLOBAL_CROPS * (q % half) + q // half).astype(bf16), t)
    s = sf[...]
    s = s / jnp.sqrt(jnp.sum(s * s, axis=1, keepdims=True) + norm_eps)
    n = s.shape[0]
    q = lax.broadcasted_iota(jnp.int32, (n, n), 0)
    s_v[...] = exact_pick((q == place[...]).astype(bf16), s)
    total = sf.shape[0] + tf.shape[0]
    few_s = sf.shape[0] * out.shape[0] // total
    few_t = out.shape[0] - few_s
    out[:few_s] = s_v[pl.ds(pl.multiple_of(turn[0] * few_s, 8), few_s)]
    out[few_s:] = t_v[pl.ds(pl.multiple_of(turn[0] * few_t, 8), few_t)]


def pieces_kernel(tp, sp, pieces, tp_v, sp_v, in_sems, out_sems):
    n_dp, _, _, cols = pieces.shape
    loads = [begin(tp, tp_v, in_sems.at[0]), begin(sp, sp_v, in_sems.at[1])]
    stores = []
    for k, src in enumerate((tp_v, sp_v)):
        loads[k].wait()
        for i in range(n_dp):
            stores.append(
                begin(src.at[:, i * cols : (i + 1) * cols], pieces.at[i, k], out_sems.at[i, k])
            )
    for copy in stores:
        copy.wait()


def assembled(turn, pieces, to, rows, skip):
    turns, blks, _, _ = pieces.shape
    few = rows // turns
    for d in range(turns):
        place = pl.multiple_of((turn[0] + d) % turns * few, 8)
        for j in range(blks):
            to(j, place, few, pieces[d, j, skip : skip + few])


def teacher_kernel(index, turn, temp, got, own, other, kt_out, part_out, t_scr):
    n_all, t_rows, width = t_scr.shape
    n_blk = n_all // 2
    skip = own.shape[2] - t_rows // own.shape[0]
    teach = got[:, 0].reshape(width, got.shape[-1])
    norm = jnp.sqrt(jnp.sum(teach * teach, axis=0, keepdims=True) + norm_eps)
    unit = (teach / norm).T
    for half, pieces in enumerate((own, other)):

        def put(j, place, few, rows):
            t_scr[index[half * n_blk + j], pl.ds(place, few)] = rows

        assembled(turn, pieces, put, t_rows, skip)
    t = t_scr[...].reshape(n_all * t_rows, width)
    kt = jnp.exp(mul3(halves(unit), halves(t), NT) / temp[0])
    kt_out[...] = kt
    col = 1.0 / jnp.sum(kt, axis=1, keepdims=True)
    part_out[...] = jnp.sum(kt * col, axis=0, keepdims=True)


def scaled_round(kt_in, got):
    kt = kt_in[...]
    row = 1.0 / jnp.sum(got[:, :, : kt.shape[1]], axis=0)
    col = 1.0 / jnp.sum(kt * row, axis=1, keepdims=True)
    return kt * col


def second_kernel(kt_in, got, part_out, tot_out):
    last = scaled_round(kt_in, got)
    part_out[...] = jnp.sum(last, axis=0, keepdims=True)
    tot_out[...] = jnp.sum(got[:, :, last.shape[1] :], axis=0)


def third_kernel(kt_in, got, part_out, last_out):
    last = scaled_round(kt_in, got)
    last_out[...] = last
    part_out[...] = jnp.sum(last, axis=0, keepdims=True)


CHUNK = 256


def expos(rows, u):
    return jnp.exp(mul3(halves(rows), u, NN) / student_temp)


def student_kernel(
    index, turn, own, other, got, part, mine, given, f_own, f_other, w_out, u_out, n_out,
    s_scr, w_scr, tot_scr,
):
    _, n_blk, _, rows = tot_scr.shape
    all_rows, width = f_own.shape
    images = rows // CROPS
    n = all_rows // CHUNK
    raw = got[:, 1].reshape(width, got.shape[-1])
    norm = jnp.sqrt(jnp.sum(raw * raw, axis=0, keepdims=True) + norm_eps)
    unit = raw / norm
    u_out[...] = unit
    n_out[...] = norm
    u, v = halves(unit), halves(unit.T)
    for half, (pieces, f_out, message) in enumerate(((own, f_own, mine), (other, f_other, given))):
        src = s_scr.at[half]

        def put(j, place, few, piece):
            src[pl.ds(place + j * rows, few)] = piece

        assembled(turn, pieces, put, rows, 0)
        line = []
        for i in range(n):
            a, b = i * CHUNK, (i + 1) * CHUNK
            expo = expos(src[a:b], u)
            lanes = expo[:, :128]
            for k in range(1, expo.shape[1] // 128):
                lanes = lanes + expo[:, 128 * k : 128 * (k + 1)]
            line.append(jnp.sum(lanes.T, axis=0, keepdims=True))
            f_out[a:b] = mul3(halves(expo), v, NN)
        line = jnp.concatenate(line, axis=1)
        for j in range(n_blk):
            to = index[half * n_blk + j]
            tot_scr[half, to % n_blk] = line[:, j * rows : (j + 1) * rows]
            by_slot = src[j * rows : (j + 1) * rows].reshape(CROPS, images, width)
            local = jnp.sum(by_slot[GLOBAL_CROPS:], axis=0)
            w_scr[to, 0] = by_slot[1] + local
            w_scr[to, 1] = by_slot[0] + local
        message[...] = jnp.concatenate([part[...]] + [tot_scr[half, j] for j in range(n_blk)], axis=1)
    w_out[...] = w_scr[...].reshape(2 * n_blk * GLOBAL_CROPS * images, width).T


def grad_kernel(
    index, turn, own, other, tot_own, tot_other, unit, g_out, s_scr, tot_scr, *, coef
):
    _, all_rows, _ = s_scr.shape
    _, n_blk, _, rows = tot_scr.shape
    n = all_rows // CHUNK
    lane = lax.broadcasted_iota(jnp.int32, (1, rows), 1)
    count = jnp.where(lane < GLOBAL_CROPS * (rows // CROPS), GLOBAL_CROPS - 1.0, GLOBAL_CROPS * 1.0)
    u = halves(unit[...])
    g = None
    for half, (pieces, tot) in enumerate(((own, tot_own), (other, tot_other))):
        src = s_scr.at[half]

        def put(j, place, few, piece):
            src[pl.ds(place + j * rows, few)] = piece

        assembled(turn, pieces, put, rows, 0)
        for j in range(n_blk):
            tot_scr[half, j] = coef * count / tot[:, j * rows : (j + 1) * rows]
        scale = jnp.concatenate(
            [tot_scr[half, index[half * n_blk + j] % n_blk] for j in range(n_blk)], axis=1
        )
        for i in range(n):
            a, b = i * CHUNK, (i + 1) * CHUNK
            x = src[a:b]
            part = mul3(halves(x.T * scale[:, a:b]), halves(expos(x, u)), NN)
            g = part if g is None else g + part
    g_out[...] = g


def back_kernel(index, last, unit, own, other, scr):
    n_blk, rows, width = own.shape
    back = mul3(halves(last[...].T), halves(unit[...].T), NN)
    scr[...] = back.reshape(2 * n_blk, rows, width)
    for j in range(n_blk):
        own[j] = scr[index[j]]
        other[j] = scr[index[n_blk + j]]


def final_kernel(
    rate, got, last, weights, g_in, raw_in, unit_in, norm_in, next_out, row_out, *, coef
):
    width, cols = g_in.shape
    row = 1.0 / jnp.sum(got[...], axis=0)
    row_out[...] = row
    pulled = mul3(halves(weights[...] * (coef * row)), halves(last[...]), NT)
    g = g_in[...] - pulled
    unit = unit_in[...]
    along = jnp.sum(unit * g, axis=0, keepdims=True)
    proto_grad = (g - unit * along) / norm_in[...]
    square = jnp.mean(proto_grad * proto_grad, axis=0, keepdims=True)
    direction = proto_grad / jnp.sqrt(square + square_eps)
    raw = raw_in[:, 1].reshape(width, cols)
    new = raw - rate[0] * (direction + weight_decay * raw)
    next_out[...] = new.reshape(next_out.shape)


def other_core(v):
    return lax.ppermute(v, "c", ((0, 1), (1, 0)))


def spread_kernel(mine, theirs, out):
    out[...] = jnp.broadcast_to((mine[...] + theirs[...])[None], out.shape)


def everywhere(mine, given):
    theirs = other_core(given)
    n = lax.axis_size(CHIPS)
    (copies,) = call(spread_kernel, [VMEM, VMEM], [(VMEM, shape(n, *mine.shape))])(mine, theirs)
    return lax.all_to_all(copies, CHIPS, split_axis=0, concat_axis=0, tiled=True)


def shifted(v, axis, by):
    n = lax.axis_size(axis)
    return lax.ppermute(v, axis, [(i, (i + by) % n) for i in range(n)])


def mirrored(v):
    return lax.ppermute(v, ("zh", "zl"), [(i, 3 - i) for i in range(4)])


def gather_turns(v):
    v = jnp.stack([v, mirrored(v)])
    v = jnp.stack([v, shifted(v, "x", 3), shifted(v, "x", 2), shifted(v, "x", 1)])
    v = jnp.stack([v, shifted(v, "y", 3), shifted(v, "y", 2), shifted(v, "y", 1)])
    return v, other_core(v)


def scatter_chips(own, other):
    v = own + other_core(other)
    v = v[0] + shifted(v[1], "x", 1) + shifted(v[2], "x", 2) + shifted(v[3], "x", 3)
    return v


def scatter_rest(v):
    v = v[0] + mirrored(v[1])
    v = v + shifted(v, "zl", 1)
    v = v + lax.ppermute(v, "y", [(i, i ^ 1) for i in range(4)])
    return v + lax.ppermute(v, "y", [(i, 3 - i) for i in range(4)])


def body(student_feats, teacher_feats, student_proto, teacher_proto, crops, step):
    rate, teacher_temp, momentum = plan(step)
    n_dp = lax.axis_size(DP)
    own_rows, own_cols = student_proto.shape
    cols = own_cols // n_dp
    width = own_rows * n_dp
    crop_rows = student_feats.shape[0]
    teach_rows = teacher_feats.shape[0]
    images = teach_rows // GLOBAL_CROPS
    all_teach = n_dp * teach_rows
    pair_total = GLOBAL_CROPS * (GLOBAL_CROPS - 1) + (CROPS - GLOBAL_CROPS) * GLOBAL_CROPS
    coef = loss_scale / (pair_total * images * n_dp * student_temp)

    core, x, zh = lax.axis_index("c"), lax.axis_index("x"), lax.axis_index("zh")
    around = jnp.arange(n_dp, dtype=jnp.int32)
    index = (around // 8 ^ core) * 8 + (around // 2 + x) % 4 * 2 + (around % 2 ^ zh)

    turn = lax.axis_index("y")[None]
    n_turn = lax.axis_size("y")
    place = crops[:, 1] * images + crops[:, 0]
    both_rows = crop_rows + teach_rows
    (rows,) = call(
        rows_kernel,
        [SMEM, VMEM, VMEM, VMEM],
        [(VMEM, shape(both_rows // n_turn, width))],
        [room_for(crop_rows, width), room_for(teach_rows, width)],
        60 * 1024,
    )(turn, place[None, :], student_feats, teacher_feats)
    (pieces,) = call(
        pieces_kernel,
        [HBM, HBM],
        [(HBM, shape(n_dp, 2, own_rows, cols))],
        [room_for(own_rows, own_cols), room_for(own_rows, own_cols), DMA((2,)), DMA((n_dp, 2))],
        60 * 1024,
    )(teacher_proto, student_proto)
    got = lax.all_to_all(pieces, DP, split_axis=0, concat_axis=0, tiled=True)
    n_blk = n_dp // 2
    own, other = (
        v.reshape(n_turn, n_blk, both_rows // n_turn, width) for v in gather_turns(rows)
    )

    kt_shape = shape(cols, all_teach)
    kt, part = call(
        teacher_kernel,
        [SMEM, SMEM, SMEM, VMEM, VMEM, VMEM],
        [(VMEM, kt_shape), (VMEM, shape(1, all_teach))],
        [room_for(n_dp, teach_rows, width)],
    )(index, turn, teacher_temp[None], got, own, other)
    half = (n_blk * crop_rows, width)
    line = (1, n_blk * crop_rows)
    message = shape(1, all_teach + line[1])
    mine, given, f_own, f_other, weights, unit, norm = call(
        student_kernel,
        [SMEM, SMEM, VMEM, VMEM, VMEM, VMEM],
        [
            (VMEM, message),
            (VMEM, message),
            (VMEM, shape(*half)),
            (VMEM, shape(*half)),
            (VMEM, shape(width, all_teach)),
            (VMEM, shape(width, cols)),
            (VMEM, shape(1, cols)),
        ],
        [
            room_for(2, *half),
            room_for(n_dp, GLOBAL_CROPS, images, width),
            room_for(2, n_blk, 1, crop_rows),
        ],
    )(index, turn, own, other, got, part)
    sums = everywhere(mine, given)
    four = (4, 2, crop_rows, width)
    mine_s = scatter_chips(f_own.reshape(four), f_other.reshape(four))
    part, tot_own = call(
        second_kernel, [VMEM, VMEM], [(VMEM, shape(1, all_teach)), (VMEM, shape(*line))]
    )(kt, sums)
    tot_other = other_core(tot_own)
    sums = everywhere(part, part)
    part, last = call(
        third_kernel, [VMEM, VMEM], [(VMEM, shape(1, all_teach)), (VMEM, kt_shape)]
    )(kt, sums)
    sums = everywhere(part, part)

    b_own, b_other = call(
        back_kernel,
        [SMEM, VMEM, VMEM],
        [(VMEM, shape(n_blk, teach_rows, width))] * 2,
        [room_for(n_dp, teach_rows, width)],
    )(index, last, unit)
    four = (4, 2, teach_rows, width)
    mine_t = scatter_chips(b_own.reshape(four), b_other.reshape(four))
    mine = scatter_rest(jnp.concatenate([mine_s, mine_t], axis=1))
    mine_s, mine_t = mine[:crop_rows], mine[crop_rows:]

    (g,) = call(
        functools.partial(grad_kernel, coef=coef),
        [SMEM, SMEM, VMEM, VMEM, VMEM, VMEM, VMEM],
        [(VMEM, shape(width, cols))],
        [room_for(2, *half), room_for(2, n_blk, 1, crop_rows)],
    )(index, turn, own, other, tot_own, tot_other, unit)
    next_cols, row = call(
        functools.partial(final_kernel, coef=coef),
        [SMEM, VMEM, VMEM, VMEM, VMEM, VMEM, VMEM, VMEM],
        [(VMEM, shape(n_dp, own_rows, cols)), (VMEM, shape(1, all_teach))],
    )(rate[None], sums, last, weights, g, got, unit, norm)
    back = lax.all_to_all(next_cols, DP, split_axis=0, concat_axis=0, tiled=True)
    student_next = back.transpose(1, 0, 2).reshape(own_rows, own_cols)
    teacher_next = momentum * teacher_proto + (1.0 - momentum) * student_next

    my_block = x * 2 + zh
    my_total = lax.dynamic_index_in_dim(tot_own.reshape(n_blk, crop_rows), my_block, 0, keepdims=False)
    my_row = lax.dynamic_index_in_dim(row.reshape(n_dp, teach_rows), core * 8 + my_block, 0, keepdims=False)
    slots = jnp.arange(crop_rows) // images
    count = jnp.where(slots < GLOBAL_CROPS, GLOBAL_CROPS - 1.0, GLOBAL_CROPS * 1.0)
    scale = coef * count / my_total
    part_t = (coef * my_row[:, None] * mine_t).reshape(GLOBAL_CROPS, images, width)
    both_t = part_t[0] + part_t[1]
    target = jnp.concatenate(
        [part_t[1][None], part_t[0][None], jnp.broadcast_to(both_t, (CROPS - GLOBAL_CROPS, *both_t.shape))]
    ).reshape(crop_rows, width)
    feature_sorted = mine_s * scale[:, None] - target
    q_iota = lax.broadcasted_iota(jnp.int32, (crop_rows, crop_rows), 0)
    sort = (q_iota == place[None, :]).astype(f32)
    feature_unit = dot(sort, feature_sorted, ((0,), (0,)), highest)
    s_norm = jnp.sqrt(jnp.sum(student_feats * student_feats, axis=1, keepdims=True) + norm_eps)
    s_unit = student_feats / s_norm
    feature_grad = (
        feature_unit - s_unit * jnp.sum(s_unit * feature_unit, axis=1, keepdims=True)
    ) / s_norm
    return (student_next, teacher_next, feature_grad)


def solution(mesh):
    n_x, n_zh, n_c, n_y, n_zl = 4, 2, 2, 4, 2
    fine = Mesh(mesh.devices.reshape(n_x, n_zh, n_c, n_y, n_zl), AXES)
    in_specs = (P(DP, None), P(DP, None), P(DP, PROTO), P(DP, PROTO), P(DP, None), P())
    out_specs = (P(DP, PROTO), P(DP, PROTO), P(DP, None))
    return jax.shard_map(body, mesh=fine, in_specs=in_specs, out_specs=out_specs, check_vma=False)
```

```python
import functools

import jax
import jax.numpy as jnp
from jax import lax
from jax.experimental import pallas as pl
from jax.experimental.pallas import tpu as pltpu
from jax.sharding import Mesh, PartitionSpec as P

CROPS = 10
GLOBAL_CROPS = 2
WARM_STEPS = 12500
TOTAL_STEPS = 625000

student_temp = 0.1
loss_scale = 16777216.0
norm_eps = 1e-06
square_eps = 1e-06
rate_peak = 0.05
weight_decay = 0.04
momentum_base = 0.994
highest = lax.Precision.HIGHEST
high = lax.Precision.HIGH
f32 = jnp.float32
bf16 = jnp.bfloat16


AXES = ("x", "zh", "c", "y", "zl")
DP = ("x", "zh", "c")
PROTO = ("y", "zl")
CHIPS = ("x", "zh", "y", "zl")


def dot(a, b, dims, precision=high):
    return lax.dot_general(a, b, (dims, ((), ())), precision=precision, preferred_element_type=f32)


def plan(step):
    value = step[0].astype(f32)
    ramp = jnp.minimum(1.0, value / WARM_STEPS)
    rate = rate_peak * (0.25 + 0.75 * ramp)
    teacher_temp = 0.04 + 0.03 * ramp
    momentum = 1.0 - (1.0 - momentum_base) * (jnp.cos(jnp.pi * value / TOTAL_STEPS) + 1.0) * 0.5
    return (rate, teacher_temp, momentum)


NN = ((1,), (0,))
NT = ((1,), (1,))


def halves(v):
    high_part = v.astype(bf16)
    return high_part, (v - high_part.astype(f32)).astype(bf16)


def mul(a, b, dims):
    return lax.dot_general(a, b, (dims, ((), ())), preferred_element_type=f32)


def mul3(a, b, dims):
    return mul(a[0], b[0], dims) + mul(a[0], b[1], dims) + mul(a[1], b[0], dims)


def exact_pick(pick, v):
    one = v.astype(bf16)
    rest = v - one.astype(f32)
    two = rest.astype(bf16)
    three = (rest - two.astype(f32)).astype(bf16)
    return mul(pick, one, NN) + mul(pick, two, NN) + mul(pick, three, NN)


VMEM = pl.BlockSpec(memory_space=pltpu.VMEM)
SMEM = pl.BlockSpec(memory_space=pltpu.SMEM)
HBM = pl.BlockSpec(memory_space=pltpu.HBM)
DMA = pltpu.SemaphoreType.DMA


def shape(*dims):
    return jax.ShapeDtypeStruct(dims, f32)


def room_for(*dims):
    return pltpu.VMEM(dims, f32)


def call(kernel, ins, outs, scratch=(), room=16000):
    return pl.pallas_call(
        kernel,
        in_specs=ins,
        out_specs=[spec for spec, _ in outs],
        out_shape=[out for _, out in outs],
        scratch_shapes=list(scratch),
        compiler_params=pltpu.CompilerParams(vmem_limit_bytes=room * 1024),
    )


def begin(src, dst, sem):
    copy = pltpu.make_async_copy(src, dst, sem)
    copy.start()
    return copy


def rows_kernel(turn, place, sf, tf, out, s_v, t_v):
    t = tf[...]
    t = t / jnp.sqrt(jnp.sum(t * t, axis=1, keepdims=True) + norm_eps)
    n = t.shape[0]
    q = lax.broadcasted_iota(jnp.int32, (n, n), 0)
    r = lax.broadcasted_iota(jnp.int32, (n, n), 1)
    half = n // GLOBAL_CROPS
    t_v[...] = exact_pick((r == GLOBAL_CROPS * (q % half) + q // half).astype(bf16), t)
    s = sf[...]
    s = s / jnp.sqrt(jnp.sum(s * s, axis=1, keepdims=True) + norm_eps)
    n = s.shape[0]
    q = lax.broadcasted_iota(jnp.int32, (n, n), 0)
    s_v[...] = exact_pick((q == place[...]).astype(bf16), s)
    total = sf.shape[0] + tf.shape[0]
    few_s = sf.shape[0] * out.shape[0] // total
    few_t = out.shape[0] - few_s
    out[:few_s] = s_v[pl.ds(pl.multiple_of(turn[0] * few_s, 8), few_s)]
    out[few_s:] = t_v[pl.ds(pl.multiple_of(turn[0] * few_t, 8), few_t)]


def pieces_kernel(tp, sp, pieces, tp_v, sp_v, in_sems, out_sems):
    n_dp, _, _, cols = pieces.shape
    loads = [begin(tp, tp_v, in_sems.at[0]), begin(sp, sp_v, in_sems.at[1])]
    stores = []
    for k, src in enumerate((tp_v, sp_v)):
        loads[k].wait()
        for i in range(n_dp):
            stores.append(
                begin(src.at[:, i * cols : (i + 1) * cols], pieces.at[i, k], out_sems.at[i, k])
            )
    for copy in stores:
        copy.wait()


def assembled(turn, pieces, to, rows, skip):
    turns, blks, _, _ = pieces.shape
    few = rows // turns
    for d in range(turns):
        place = pl.multiple_of((turn[0] + d) % turns * few, 8)
        for j in range(blks):
            to(j, place, few, pieces[d, j, skip : skip + few])


def teacher_kernel(index, turn, temp, got, own, other, kt_out, part_out, t_scr):
    n_all, t_rows, width = t_scr.shape
    n_blk = n_all // 2
    skip = own.shape[2] - t_rows // own.shape[0]
    teach = got[:, 0].reshape(width, got.shape[-1])
    norm = jnp.sqrt(jnp.sum(teach * teach, axis=0, keepdims=True) + norm_eps)
    unit = (teach / norm).T
    for half, pieces in enumerate((own, other)):

        def put(j, place, few, rows):
            t_scr[index[half * n_blk + j], pl.ds(place, few)] = rows

        assembled(turn, pieces, put, t_rows, skip)
    t = t_scr[...].reshape(n_all * t_rows, width)
    kt = jnp.exp(mul3(halves(unit), halves(t), NT) / temp[0])
    kt_out[...] = kt
    col = 1.0 / jnp.sum(kt, axis=1, keepdims=True)
    part_out[...] = jnp.sum(kt * col, axis=0, keepdims=True)


def scaled_round(kt_in, got):
    kt = kt_in[...]
    row = 1.0 / jnp.sum(got[:, :, : kt.shape[1]], axis=0)
    col = 1.0 / jnp.sum(kt * row, axis=1, keepdims=True)
    return kt * col


def second_kernel(kt_in, got, part_out, tot_out):
    last = scaled_round(kt_in, got)
    part_out[...] = jnp.sum(last, axis=0, keepdims=True)
    tot_out[...] = jnp.sum(got[:, :, last.shape[1] :], axis=0)


def third_kernel(kt_in, got, part_out, last_out):
    last = scaled_round(kt_in, got)
    last_out[...] = last
    part_out[...] = jnp.sum(last, axis=0, keepdims=True)


CHUNK = 256


def expos(rows, u):
    return jnp.exp(mul3(halves(rows), u, NN) / student_temp)


def student_kernel(
    index, turn, own, other, got, part, mine, given, f_own, f_other, w_out, u_out, n_out,
    s_scr, w_scr, tot_scr,
):
    _, n_blk, _, rows = tot_scr.shape
    all_rows, width = f_own.shape
    images = rows // CROPS
    n = all_rows // CHUNK
    raw = got[:, 1].reshape(width, got.shape[-1])
    norm = jnp.sqrt(jnp.sum(raw * raw, axis=0, keepdims=True) + norm_eps)
    unit = raw / norm
    u_out[...] = unit
    n_out[...] = norm
    u, v = halves(unit), halves(unit.T)
    for half, (pieces, f_out, message) in enumerate(((own, f_own, mine), (other, f_other, given))):
        src = s_scr.at[half]

        def put(j, place, few, piece):
            src[pl.ds(place + j * rows, few)] = piece

        assembled(turn, pieces, put, rows, 0)
        line = []
        for i in range(n):
            a, b = i * CHUNK, (i + 1) * CHUNK
            expo = expos(src[a:b], u)
            lanes = expo[:, :128]
            for k in range(1, expo.shape[1] // 128):
                lanes = lanes + expo[:, 128 * k : 128 * (k + 1)]
            line.append(jnp.sum(lanes.T, axis=0, keepdims=True))
            f_out[a:b] = mul3(halves(expo), v, NN)
        line = jnp.concatenate(line, axis=1)
        for j in range(n_blk):
            to = index[half * n_blk + j]
            tot_scr[half, to % n_blk] = line[:, j * rows : (j + 1) * rows]
            by_slot = src[j * rows : (j + 1) * rows].reshape(CROPS, images, width)
            local = jnp.sum(by_slot[GLOBAL_CROPS:], axis=0)
            w_scr[to, 0] = by_slot[1] + local
            w_scr[to, 1] = by_slot[0] + local
        message[...] = jnp.concatenate([part[...]] + [tot_scr[half, j] for j in range(n_blk)], axis=1)
    w_out[...] = w_scr[...].reshape(2 * n_blk * GLOBAL_CROPS * images, width).T


def grad_kernel(
    index, turn, own, other, tot_own, tot_other, unit, g_out, s_scr, tot_scr, *, coef
):
    _, all_rows, _ = s_scr.shape
    _, n_blk, _, rows = tot_scr.shape
    n = all_rows // CHUNK
    lane = lax.broadcasted_iota(jnp.int32, (1, rows), 1)
    count = jnp.where(lane < GLOBAL_CROPS * (rows // CROPS), GLOBAL_CROPS - 1.0, GLOBAL_CROPS * 1.0)
    u = halves(unit[...])
    g = None
    for half, (pieces, tot) in enumerate(((own, tot_own), (other, tot_other))):
        src = s_scr.at[half]

        def put(j, place, few, piece):
            src[pl.ds(place + j * rows, few)] = piece

        assembled(turn, pieces, put, rows, 0)
        for j in range(n_blk):
            tot_scr[half, j] = coef * count / tot[:, j * rows : (j + 1) * rows]
        scale = jnp.concatenate(
            [tot_scr[half, index[half * n_blk + j] % n_blk] for j in range(n_blk)], axis=1
        )
        for i in range(n):
            a, b = i * CHUNK, (i + 1) * CHUNK
            x = src[a:b]
            part = mul3(halves(x.T * scale[:, a:b]), halves(expos(x, u)), NN)
            g = part if g is None else g + part
    g_out[...] = g


def back_kernel(index, last, unit, own, other, scr):
    n_blk, rows, width = own.shape
    back = mul3(halves(last[...].T), halves(unit[...].T), NN)
    scr[...] = back.reshape(2 * n_blk, rows, width)
    for j in range(n_blk):
        own[j] = scr[index[j]]
        other[j] = scr[index[n_blk + j]]


def final_kernel(
    rate, got, last, weights, g_in, raw_in, unit_in, norm_in, next_out, row_out, *, coef
):
    width, cols = g_in.shape
    row = 1.0 / jnp.sum(got[...], axis=0)
    row_out[...] = row
    pulled = mul3(halves(weights[...] * (coef * row)), halves(last[...]), NT)
    g = g_in[...] - pulled
    unit = unit_in[...]
    along = jnp.sum(unit * g, axis=0, keepdims=True)
    proto_grad = (g - unit * along) / norm_in[...]
    square = jnp.mean(proto_grad * proto_grad, axis=0, keepdims=True)
    direction = proto_grad / jnp.sqrt(square + square_eps)
    raw = raw_in[:, 1].reshape(width, cols)
    new = raw - rate[0] * (direction + weight_decay * raw)
    next_out[...] = new.reshape(next_out.shape)


def other_core(v):
    return lax.ppermute(v, "c", ((0, 1), (1, 0)))


def spread_kernel(mine, theirs, out):
    out[...] = jnp.broadcast_to((mine[...] + theirs[...])[None], out.shape)


def everywhere(mine, given):
    theirs = other_core(given)
    n = lax.axis_size(CHIPS)
    (copies,) = call(spread_kernel, [VMEM, VMEM], [(VMEM, shape(n, *mine.shape))])(mine, theirs)
    return lax.all_to_all(copies, CHIPS, split_axis=0, concat_axis=0, tiled=True)


def shifted(v, axis, by):
    n = lax.axis_size(axis)
    return lax.ppermute(v, axis, [(i, (i + by) % n) for i in range(n)])


def mirrored(v):
    return lax.ppermute(v, ("zh", "zl"), [(i, 3 - i) for i in range(4)])


def gather_turns(v):
    v = jnp.stack([v, mirrored(v)])
    v = jnp.stack([v, shifted(v, "x", 3), shifted(v, "x", 2), shifted(v, "x", 1)])
    v = jnp.stack([v, shifted(v, "y", 3), shifted(v, "y", 2), shifted(v, "y", 1)])
    return v, other_core(v)


def scatter_chips(own, other):
    v = own + other_core(other)
    v = v[0] + shifted(v[1], "x", 1) + shifted(v[2], "x", 2) + shifted(v[3], "x", 3)
    return v


def scatter_rest(v):
    v = v[0] + mirrored(v[1])
    v = v + shifted(v, "zl", 1)
    v = v + lax.ppermute(v, "y", [(i, i ^ 1) for i in range(4)])
    return v + lax.ppermute(v, "y", [(i, 3 - i) for i in range(4)])


def body(student_feats, teacher_feats, student_proto, teacher_proto, crops, step):
    rate, teacher_temp, momentum = plan(step)
    n_dp = lax.axis_size(DP)
    own_rows, own_cols = student_proto.shape
    cols = own_cols // n_dp
    width = own_rows * n_dp
    crop_rows = student_feats.shape[0]
    teach_rows = teacher_feats.shape[0]
    images = teach_rows // GLOBAL_CROPS
    all_teach = n_dp * teach_rows
    pair_total = GLOBAL_CROPS * (GLOBAL_CROPS - 1) + (CROPS - GLOBAL_CROPS) * GLOBAL_CROPS
    coef = loss_scale / (pair_total * images * n_dp * student_temp)

    core, x, zh = lax.axis_index("c"), lax.axis_index("x"), lax.axis_index("zh")
    around = jnp.arange(n_dp, dtype=jnp.int32)
    index = (around // 8 ^ core) * 8 + (around // 2 + x) % 4 * 2 + (around % 2 ^ zh)

    turn = lax.axis_index("y")[None]
    n_turn = lax.axis_size("y")
    place = crops[:, 1] * images + crops[:, 0]
    both_rows = crop_rows + teach_rows
    (rows,) = call(
        rows_kernel,
        [SMEM, VMEM, VMEM, VMEM],
        [(VMEM, shape(both_rows // n_turn, width))],
        [room_for(crop_rows, width), room_for(teach_rows, width)],
        60 * 1024,
    )(turn, place[None, :], student_feats, teacher_feats)
    (pieces,) = call(
        pieces_kernel,
        [HBM, HBM],
        [(HBM, shape(n_dp, 2, own_rows, cols))],
        [room_for(own_rows, own_cols), room_for(own_rows, own_cols), DMA((2,)), DMA((n_dp, 2))],
        60 * 1024,
    )(teacher_proto, student_proto)
    got = lax.all_to_all(pieces, DP, split_axis=0, concat_axis=0, tiled=True)
    n_blk = n_dp // 2
    own, other = (
        v.reshape(n_turn, n_blk, both_rows // n_turn, width) for v in gather_turns(rows)
    )

    kt_shape = shape(cols, all_teach)
    kt, part = call(
        teacher_kernel,
        [SMEM, SMEM, SMEM, VMEM, VMEM, VMEM],
        [(VMEM, kt_shape), (VMEM, shape(1, all_teach))],
        [room_for(n_dp, teach_rows, width)],
    )(index, turn, teacher_temp[None], got, own, other)
    half = (n_blk * crop_rows, width)
    line = (1, n_blk * crop_rows)
    message = shape(1, all_teach + line[1])
    mine, given, f_own, f_other, weights, unit, norm = call(
        student_kernel,
        [SMEM, SMEM, VMEM, VMEM, VMEM, VMEM],
        [
            (VMEM, message),
            (VMEM, message),
            (VMEM, shape(*half)),
            (VMEM, shape(*half)),
            (VMEM, shape(width, all_teach)),
            (VMEM, shape(width, cols)),
            (VMEM, shape(1, cols)),
        ],
        [
            room_for(2, *half),
            room_for(n_dp, GLOBAL_CROPS, images, width),
            room_for(2, n_blk, 1, crop_rows),
        ],
        60 * 1024,
    )(index, turn, own, other, got, part)
    sums = everywhere(mine, given)
    four = (4, 2, crop_rows, width)
    mine_s = scatter_chips(f_own.reshape(four), f_other.reshape(four))
    part, tot_own = call(
        second_kernel, [VMEM, VMEM], [(VMEM, shape(1, all_teach)), (VMEM, shape(*line))], (), 60 * 1024
    )(kt, sums)
    tot_other = other_core(tot_own)
    sums = everywhere(part, part)
    part, last = call(
        third_kernel, [VMEM, VMEM], [(VMEM, shape(1, all_teach)), (VMEM, kt_shape)]
    )(kt, sums)
    sums = everywhere(part, part)

    b_own, b_other = call(
        back_kernel,
        [SMEM, VMEM, VMEM],
        [(VMEM, shape(n_blk, teach_rows, width))] * 2,
        [room_for(n_dp, teach_rows, width)],
    )(index, last, unit)
    four = (4, 2, teach_rows, width)
    mine_t = scatter_chips(b_own.reshape(four), b_other.reshape(four))
    mine = scatter_rest(jnp.concatenate([mine_s, mine_t], axis=1))
    mine_s, mine_t = mine[:crop_rows], mine[crop_rows:]

    (g,) = call(
        functools.partial(grad_kernel, coef=coef),
        [SMEM, SMEM, VMEM, VMEM, VMEM, VMEM, VMEM],
        [(VMEM, shape(width, cols))],
        [room_for(2, *half), room_for(2, n_blk, 1, crop_rows)],
        60 * 1024,
    )(index, turn, own, other, tot_own, tot_other, unit)
    next_cols, row = call(
        functools.partial(final_kernel, coef=coef),
        [SMEM, VMEM, VMEM, VMEM, VMEM, VMEM, VMEM, VMEM],
        [(VMEM, shape(n_dp, own_rows, cols)), (VMEM, shape(1, all_teach))],
        (),
        60 * 1024,
    )(rate[None], sums, last, weights, g, got, unit, norm)
    back = lax.all_to_all(next_cols, DP, split_axis=0, concat_axis=0, tiled=True)
    student_next = back.transpose(1, 0, 2).reshape(own_rows, own_cols)
    teacher_next = momentum * teacher_proto + (1.0 - momentum) * student_next

    my_block = x * 2 + zh
    my_total = lax.dynamic_index_in_dim(tot_own.reshape(n_blk, crop_rows), my_block, 0, keepdims=False)
    my_row = lax.dynamic_index_in_dim(row.reshape(n_dp, teach_rows), core * 8 + my_block, 0, keepdims=False)
    slots = jnp.arange(crop_rows) // images
    count = jnp.where(slots < GLOBAL_CROPS, GLOBAL_CROPS - 1.0, GLOBAL_CROPS * 1.0)
    scale = coef * count / my_total
    part_t = (coef * my_row[:, None] * mine_t).reshape(GLOBAL_CROPS, images, width)
    both_t = part_t[0] + part_t[1]
    target = jnp.concatenate(
        [part_t[1][None], part_t[0][None], jnp.broadcast_to(both_t, (CROPS - GLOBAL_CROPS, *both_t.shape))]
    ).reshape(crop_rows, width)
    feature_sorted = mine_s * scale[:, None] - target
    q_iota = lax.broadcasted_iota(jnp.int32, (crop_rows, crop_rows), 0)
    sort = (q_iota == place[None, :]).astype(f32)
    feature_unit = dot(sort, feature_sorted, ((0,), (0,)), highest)
    s_norm = jnp.sqrt(jnp.sum(student_feats * student_feats, axis=1, keepdims=True) + norm_eps)
    s_unit = student_feats / s_norm
    feature_grad = (
        feature_unit - s_unit * jnp.sum(s_unit * feature_unit, axis=1, keepdims=True)
    ) / s_norm
    return (student_next, teacher_next, feature_grad)


def solution(mesh):
    n_x, n_zh, n_c, n_y, n_zl = 4, 2, 2, 4, 2
    fine = Mesh(mesh.devices.reshape(n_x, n_zh, n_c, n_y, n_zl), AXES)
    in_specs = (P(DP, None), P(DP, None), P(DP, PROTO), P(DP, PROTO), P(DP, None), P())
    out_specs = (P(DP, PROTO), P(DP, PROTO), P(DP, None))
    return jax.shard_map(body, mesh=fine, in_specs=in_specs, out_specs=out_specs, check_vma=False)
```
